128 devices in a mesh: frm: 8 (over z, core), vox: 16 (over y, x).
Axes of the slice: x: 4, y: 4, z: 4, core: 2. Of those that a mesh axis runs over, the one named last changes fastest.
Arguments:
- movie_matrix: bfloat16 [16384, 32768], P('frm', 'vox'), may hold values from -8 to 8
- voxel_probe: bfloat16 [32768, 64], P('vox'), may hold values from -0.03125 to 0.03125
- frame_probe: bfloat16 [16384, 64], P('frm'), may hold values from -0.046875 to 0.046875
Outputs:
- lowrank: bfloat16 [16384, 32768], P('frm', 'vox')
- sparse: bfloat16 [16384, 32768], P('frm', 'vox')
The draws below stay inside these ranges and needn't reach their ends.
All inputs are finite; a program needn't handle non-finite values.
Results may differ from the reference program's by a relative error of at most 0.04.
Values may be sent and summed in bfloat16 or wider, within the bound.
A program may use at most 128 MiB of HBM per device.

```python
import jax
import jax.numpy as jnp
from jax import lax

RANK = 64
ITERS = 2
FRAMES = 16384
VOXELS = 32768


signal_rank = 96


def draw_movie_matrix(key, part):
    keys = jax.random.split(jax.random.fold_in(key, 17), 6)
    basis_left = jax.random.normal(keys[0], (FRAMES, signal_rank), jnp.float32)
    basis_right = jax.random.normal(keys[1], (VOXELS, signal_rank), jnp.float32)
    signal = jnp.dot(basis_left, basis_right.T, precision=lax.Precision.HIGHEST) / jnp.sqrt(float(signal_rank))
    spike_mask = jax.random.bernoulli(keys[2], 0.05, (FRAMES, VOXELS)).astype(jnp.float32)
    spike_sign = 2.0 * jax.random.bernoulli(keys[3], 0.5, (FRAMES, VOXELS)).astype(jnp.float32) - 1.0
    spike_size = jax.random.uniform(keys[4], (FRAMES, VOXELS), jnp.float32, 2.0, 4.0)
    noise = 0.3 * jax.random.normal(keys[5], (FRAMES, VOXELS), jnp.float32)
    movie = signal + noise + spike_mask * spike_sign * spike_size
    return jnp.clip(movie, -8.0, 8.0).astype(jnp.bfloat16)


def level_of(own_key, extent, cuts, low, top_value):
    gain, own = 1.0, jax.random.fold_in(own_key, 6)
    for dim, shards_of in cuts:
        heights = jnp.exp(jax.random.uniform(jax.random.fold_in(own, dim), (shards_of,), jnp.float32, low / len(cuts), top_value / len(cuts)))
        gain = gain * jnp.repeat(heights, extent[dim] // shards_of).reshape([-1 if axis == dim else 1 for axis in range(len(extent))])
    return gain


def normal_values(own_key, extent, scale, limit, cuts=(), kind=jnp.bfloat16):
    drawn = scale * jax.random.normal(own_key, extent, jnp.float32)
    if cuts:
        drawn = drawn * level_of(own_key, extent, cuts, -0.22, 0.18)
    return jnp.clip(drawn, -limit, limit).astype(kind)


def setup_inputs(seed: int = 0) -> dict:
    seeds = jax.random.split(jax.random.key(seed), 4)
    return {
        "movie_matrix": draw_movie_matrix(jax.random.fold_in(seeds[3], 71), 0),
        "voxel_probe": normal_values(seeds[1], (VOXELS, RANK), VOXELS ** -0.5, 0.03125, ((0, 16),)),
        "frame_probe": normal_values(seeds[2], (FRAMES, RANK), FRAMES ** -0.5, 0.046875, ((0, 8),)),
    }


cutoff = 1.0
ridge_scale = 0.1

def core_map(core_matrix):
    gram_matrix = jnp.dot(core_matrix.T.astype(jnp.float32), core_matrix.astype(jnp.float32), precision=lax.Precision.HIGHEST, preferred_element_type=jnp.float32)
    core_order = core_matrix.shape[0]
    ridge_shift = ridge_scale * (jnp.trace(gram_matrix) / core_order + 1e-06)
    factor = jnp.linalg.cholesky(gram_matrix + ridge_shift * jnp.eye(core_order, dtype=jnp.float32))
    return jax.scipy.linalg.cho_solve((factor, True), core_matrix.T)

def shrink(values):
    return jnp.sign(values) * jnp.maximum(jnp.abs(values) - cutoff, 0.0)

def reference(movie_matrix, voxel_probe, frame_probe):
    sparse = jnp.zeros_like(movie_matrix)
    probe_wide = frame_probe.astype(jnp.float32)
    lowrank = jnp.zeros(movie_matrix.shape, jnp.float32)
    for iteration in range(ITERS):
        current = (movie_matrix.astype(jnp.float32) - sparse.astype(jnp.float32)).astype(jnp.bfloat16)
        frame_sketch = jnp.dot(current.astype(jnp.float32), voxel_probe.astype(jnp.float32), preferred_element_type=jnp.float32)
        voxel_sketch = lax.dot_general(current.astype(jnp.float32), frame_probe.astype(jnp.float32), (((0,), (0,)), ((), ())), preferred_element_type=jnp.float32)
        core_matrix = lax.dot_general(probe_wide.astype(jnp.float32), frame_sketch.astype(jnp.float32), (((0,), (0,)), ((), ())), precision=lax.Precision.HIGHEST, preferred_element_type=jnp.float32)
        core_mixer = core_map(core_matrix)
        left_factor = jnp.dot(frame_sketch.astype(jnp.float32), core_mixer.astype(jnp.float32), precision=lax.Precision.HIGHEST, preferred_element_type=jnp.float32).astype(jnp.bfloat16)
        right_factor = voxel_sketch.astype(jnp.bfloat16)
        lowrank = lax.dot_general(left_factor.astype(jnp.float32), right_factor.astype(jnp.float32), (((1,), (1,)), ((), ())), preferred_element_type=jnp.float32)
        sparse = shrink(movie_matrix.astype(jnp.float32) - lowrank).astype(jnp.bfloat16)
    return (lowrank.astype(jnp.bfloat16), sparse)
```

```python
import functools

import jax
import jax.numpy as jnp
from jax import lax
from jax.experimental import pallas as pl
from jax.experimental.pallas import tpu as pltpu
from jax.sharding import PartitionSpec as P

MESH = pl.DeviceIdType.MESH
BF16, F32 = jnp.bfloat16, jnp.float32
ITERS = 2
RANK = 64
LANES = 128
cutoff = 1.0
ridge_scale = 0.1
NN = (((1,), (0,)), ((), ()))
NT = (((1,), (1,)), ((), ()))
TN = (((0,), (0,)), ((), ()))


def mm(a, b, dims):
    return lax.dot_general(a, b, dims, preferred_element_type=F32)


def split(x):
    high = x.astype(BF16)
    return high, (x - high.astype(F32)).astype(BF16)


def solve(blocks):
    row_id = lax.broadcasted_iota(jnp.int32, (8, LANES), 0)

    def step(_, blocks):
        panel = blocks[0]
        for k in range(8):
            column, row = panel[:, k : k + 1], panel[k : k + 1, :]
            row = row / panel[k : k + 1, k : k + 1]
            panel = jnp.where(row_id == k, row, panel - column * row)
        others = []
        for block in blocks[1:]:
            for k in range(8):
                block = block - blocks_column(block, k) * panel[k : k + 1, :]
            others.append(pltpu.roll(block, LANES - 8, 1))
        return (*others, pltpu.roll(panel, LANES - 8, 1))

    def blocks_column(block, k):
        return block[:, k : k + 1]

    return lax.fori_loop(0, len(blocks), step, tuple(blocks))


def square(t):
    first, rest = t.astype(BF16), t - t.astype(BF16).astype(F32)
    second, third = rest.astype(BF16), (rest - rest.astype(BF16).astype(F32)).astype(BF16)
    tall = [jnp.concatenate([x, jnp.zeros_like(x)], axis=0) for x in (first, second, third)]
    small = mm(first, tall[2], NT) + mm(third, tall[0], NT) + mm(second, tall[1], NT)
    return small + (mm(first, tall[1], NT) + mm(second, tall[0], NT)) + mm(first, tall[0], NT)


def mixer_of(t):
    order = RANK
    gram = square(t)
    shift = ridge_scale * (jnp.sum(t * t) / order + 1e-06)
    rows = lax.broadcasted_iota(jnp.int32, t.shape, 0)
    lanes = lax.broadcasted_iota(jnp.int32, t.shape, 1)
    wide = gram + t + jnp.where(rows == lanes, shift, 0.0)
    blocks = solve([wide[8 * b : 8 * b + 8] for b in range(order // 8)])
    return jnp.concatenate(blocks, axis=0)[:, :order]


def sketch_kernel(
    nv, nf,
    m_hbm, vpt, fpt, ft_out, w_out,
    m_buf, f_send, f_recv, ft_full, v_send, v_recv, vt_full, t_acc, t_send, t_recv, t_sum, t_wide, t_full, w_buf, mix,
    m_sem, f_sem, fg_sem, v_sem, vg_sem, ta_sem, tb_sem, tc_sem,
):
    mv, mf = lax.axis_index("vox"), lax.axis_index("frm")
    frames, voxels = m_buf.shape
    fb, vb = frames // nv, voxels // nf
    rows = 2 * fb
    chunks = nv // 2

    def chunk_of(s):
        return lax.rem(mv // 2 + 1 + s, chunks)

    def rows_of(c):
        return pl.ds(pl.multiple_of(c * rows, rows), rows)

    def load(s):
        c = chunk_of(s)
        return pltpu.make_async_copy(m_hbm.at[rows_of(c)], m_buf.at[rows_of(c)], m_sem.at[s])

    for s in range(chunks):
        load(s).start()

    barrier = pltpu.get_barrier_semaphore()
    for d in range(1, nv):
        pl.semaphore_signal(barrier, inc=1, device_id={"vox": lax.rem(mv + d, nv)}, device_id_type=MESH)
    for d in range(1, nf):
        pl.semaphore_signal(barrier, inc=1, device_id={"frm": lax.rem(mf + d, nf)}, device_id_type=MESH)

    pl.semaphore_wait(barrier, nv + nf - 2)

    def to_vox(src, dst, sems, it, target):
        return pltpu.make_async_remote_copy(
            src_ref=src, dst_ref=dst, send_sem=sems.at[it, 0], recv_sem=sems.at[it, 1],
            device_id={"vox": target}, device_id_type=MESH,
        )

    def to_frm(src, dst, sems, it, target):
        return pltpu.make_async_remote_copy(
            src_ref=src, dst_ref=dst, send_sem=sems.at[it, 0], recv_sem=sems.at[it, 1],
            device_id={"frm": target}, device_id_type=MESH,
        )

    def all_of(ref, sems, it, axis, me, size):
        target = lax.rem(me + 1, size)
        return (to_vox if axis == "vox" else to_frm)(ref, ref, sems, it, target)

    for it in range(ITERS):
        t_acc[...] = jnp.zeros_like(t_acc)

        def frame_step(s, carry):
            c = chunk_of(s)
            if it == 0:
                load(s).wait()
            else:
                fblock = jnp.concatenate([ft_full[it - 1, 2 * c], ft_full[it - 1, 2 * c + 1]], axis=1)
                for j in range(nf):
                    cols = pl.ds(j * vb, vb)
                    low = mm(fblock, w_buf[:, cols], TN)
                    m = m_buf[rows_of(c), cols]
                    floor, roof = (low - cutoff).astype(BF16), (low + cutoff).astype(BF16)
                    m_buf[rows_of(c), cols] = jnp.minimum(jnp.maximum(m, floor), roof)
            ft = mm(vpt[...], m_buf[rows_of(c), :], NT)
            high, low_part = split(ft)
            f_send[it, 2 * c] = high[:, :fb]
            f_send[it, 2 * c + 1] = high[:, fb:]
            probe = fpt[:, rows_of(c)]
            t_acc[...] += mm(high, probe, NT) + mm(low_part, probe, NT)
            for h in range(2):
                owner = 2 * c + h

                @pl.when(owner != mv)
                def _():
                    slot = lax.rem(owner - mv + nv, nv) - 1
                    to_vox(f_send.at[it, owner], f_recv.at[it, slot], f_sem, it, owner).start()

            return carry

        lax.fori_loop(0, chunks, frame_step, 0)

        t = jnp.concatenate([jnp.zeros_like(t_acc), t_acc[...]], axis=1)
        for b in range(nf):
            t_send[it, b] = t[8 * b : 8 * b + 8]
        for d in range(1, nf):
            target = lax.rem(mf + d, nf)
            to_frm(t_send.at[it, target], t_recv.at[it, d - 1], ta_sem, it, target).start()

        def voxel_step(s, carry):
            c = lax.rem(mf + 1 + s, nf)
            cols = pl.ds(pl.multiple_of(c * vb, vb), vb)
            vt = mm(fpt[...], m_buf[:, cols], NN)
            v_send[it, c] = vt.astype(BF16)

            @pl.when(c != mf)
            def _():
                slot = lax.rem(c - mf + nf, nf) - 1
                to_frm(v_send.at[it, c], v_recv.at[it, slot], v_sem, it, c).start()

            return carry

        third = nf // 4
        lax.fori_loop(0, third, voxel_step, 0)

        all_of(t_recv.at[it], ta_sem, it, "frm", mf, nf).wait_recv()
        part = t_send[it, mf]
        for d in range(nf - 1):
            part = part + t_recv[it, d]
        t_sum[it] = part
        for d in range(1, nv):
            to_vox(t_sum.at[it], t_wide.at[it, d - 1], tb_sem, it, lax.rem(mv + d, nv)).start()

        lax.fori_loop(third, 2 * third, voxel_step, 0)

        all_of(f_recv.at[it], f_sem, it, "vox", mv, nv).wait_recv()
        share = f_send[it, mv].astype(F32)
        for d in range(nv - 1):
            share = share + f_recv[it, d].astype(F32)
        ft_full[it, mv] = share.astype(BF16)
        for d in range(1, nv):
            to_vox(ft_full.at[it, mv], ft_full.at[it, mv], fg_sem, it, lax.rem(mv + d, nv)).start()

        lax.fori_loop(2 * third, 3 * third, voxel_step, 0)

        all_of(t_wide.at[it], tb_sem, it, "vox", mv, nv).wait_recv()
        part = t_sum[it]
        for d in range(nv - 1):
            part = part + t_wide[it, d]
        t_full[it, mf] = part
        for d in range(1, nf):
            to_frm(t_full.at[it, mf], t_full.at[it, mf], tc_sem, it, lax.rem(mf + d, nf)).start()

        lax.fori_loop(3 * third, nf, voxel_step, 0)

        all_of(v_recv.at[it], v_sem, it, "frm", mf, nf).wait_recv()
        share = v_send[it, mf].astype(F32)
        for d in range(nf - 1):
            share = share + v_recv[it, d].astype(F32)
        vt_full[it, mf] = share.astype(BF16)
        for d in range(1, nf):
            to_frm(vt_full.at[it, mf], vt_full.at[it, mf], vg_sem, it, lax.rem(mf + d, nf)).start()

        all_of(t_full.at[it, pl.ds(0, nf - 1)], tc_sem, it, "frm", mf, nf).wait_recv()
        mixer = mixer_of(jnp.concatenate([t_full[it, b] for b in range(nf)], axis=0))
        mix[0], mix[1] = split(mixer)

        all_of(vt_full.at[it, pl.ds(0, nf - 1)], vg_sem, it, "frm", mf, nf).wait_recv()
        for b in range(nf):
            right = vt_full[it, b]
            w = mm(mix[0], right, NN) + mm(mix[1], right, NN)
            w_buf[:, b * vb : (b + 1) * vb] = w.astype(BF16)
        all_of(ft_full.at[it, pl.ds(0, nv - 1)], fg_sem, it, "vox", mv, nv).wait_recv()

    ft_out[...] = ft_full[ITERS - 1]
    w_out[...] = w_buf[...]
    for it in range(ITERS):
        all_of(f_recv.at[it], f_sem, it, "vox", mv, nv).wait_send()
        all_of(ft_full.at[it, pl.ds(0, nv - 1)], fg_sem, it, "vox", mv, nv).wait_send()
        all_of(v_recv.at[it], v_sem, it, "frm", mf, nf).wait_send()
        all_of(vt_full.at[it, pl.ds(0, nf - 1)], vg_sem, it, "frm", mf, nf).wait_send()
        all_of(t_recv.at[it], ta_sem, it, "frm", mf, nf).wait_send()
        all_of(t_wide.at[it], tb_sem, it, "vox", mv, nv).wait_send()
        all_of(t_full.at[it, pl.ds(0, nf - 1)], tc_sem, it, "frm", mf, nf).wait_send()


def output_kernel(m_ref, ft_ref, w_ref, low_ref, sparse_ref):
    fblock = jnp.concatenate([ft_ref[i] for i in range(ft_ref.shape[0])], axis=1)
    width = 256
    for j in range(m_ref.shape[1] // width):
        cols = pl.ds(j * width, width)
        low = mm(fblock, w_ref[:, cols], TN)
        rest = m_ref[:, cols].astype(F32) - low
        low_ref[:, cols] = low.astype(BF16)
        sparse_ref[:, cols] = (rest - jnp.clip(rest, -cutoff, cutoff)).astype(BF16)


def solution(mesh):
    nv, nf = mesh.shape["vox"], mesh.shape["frm"]

    def on_device(movie_matrix, voxel_probe, frame_probe):
        frames, voxels = movie_matrix.shape
        fb, vb = frames // nv, voxels // nf
        vmem = pl.BlockSpec(memory_space=pltpu.VMEM)
        dma = pltpu.SemaphoreType.DMA
        ft, w = pl.pallas_call(
            functools.partial(sketch_kernel, nv, nf),
            out_shape=(
                jax.ShapeDtypeStruct((nv, RANK, fb), BF16),
                jax.ShapeDtypeStruct((RANK, voxels), BF16),
            ),
            in_specs=[pl.BlockSpec(memory_space=pltpu.HBM), vmem, vmem],
            out_specs=(vmem, vmem),
            scratch_shapes=[
                pltpu.VMEM((frames, voxels), BF16),
                pltpu.VMEM((ITERS, nv, RANK, fb), BF16),
                pltpu.VMEM((ITERS, nv - 1, RANK, fb), BF16),
                pltpu.VMEM((ITERS, nv, RANK, fb), BF16),
                pltpu.VMEM((ITERS, nf, RANK, vb), BF16),
                pltpu.VMEM((ITERS, nf - 1, RANK, vb), BF16),
                pltpu.VMEM((ITERS, nf, RANK, vb), BF16),
                pltpu.VMEM((RANK, RANK), F32),
                pltpu.VMEM((ITERS, nf, 8, LANES), F32),
                pltpu.VMEM((ITERS, nf - 1, 8, LANES), F32),
                pltpu.VMEM((ITERS, 8, LANES), F32),
                pltpu.VMEM((ITERS, nv - 1, 8, LANES), F32),
                pltpu.VMEM((ITERS, nf, 8, LANES), F32),
                pltpu.VMEM((RANK, voxels), BF16),
                pltpu.VMEM((2, RANK, RANK), BF16),
                dma((nv // 2,)),
            ]
            + [dma((ITERS, 2))] * 7,
            compiler_params=pltpu.CompilerParams(
                collective_id=0, has_side_effects=True, vmem_limit_bytes=40 * 1024 * 1024
            ),
            name="sketches",
        )(movie_matrix, voxel_probe.T, frame_probe.T)
        per = 2
        rows = per * fb
        return pl.pallas_call(
            output_kernel,
            grid=(frames // rows,),
            out_shape=(
                jax.ShapeDtypeStruct((frames, voxels), BF16),
                jax.ShapeDtypeStruct((frames, voxels), BF16),
            ),
            in_specs=[
                pl.BlockSpec((rows, voxels), lambda i: (i, 0)),
                pl.BlockSpec((per, RANK, fb), lambda i: (i, 0, 0)),
                pl.BlockSpec((RANK, voxels), lambda i: (0, 0)),
            ],
            out_specs=(
                pl.BlockSpec((rows, voxels), lambda i: (i, 0)),
                pl.BlockSpec((rows, voxels), lambda i: (i, 0)),
            ),
            compiler_params=pltpu.CompilerParams(vmem_limit_bytes=24 * 1024 * 1024),
            name="outputs",
        )(movie_matrix, ft, w)

    return jax.shard_map(
        on_device,
        mesh=mesh,
        in_specs=(P("frm", "vox"), P("vox", None), P("frm", None)),
        out_specs=(P("frm", "vox"), P("frm", "vox")),
        check_vma=False,
    )
```

```python
import functools

import jax
import jax.numpy as jnp
from jax import lax
from jax.experimental import pallas as pl
from jax.experimental.pallas import tpu as pltpu
from jax.sharding import PartitionSpec as P

MESH = pl.DeviceIdType.MESH
BF16, F32 = jnp.bfloat16, jnp.float32
ITERS = 2
RANK = 64
HALF = RANK // 2
SUB, LANES = 8, 128
cutoff = 1.0
ridge_scale = 0.1
NN = (((1,), (0,)), ((), ()))
NT = (((1,), (1,)), ((), ()))


def mm(a, b, dims):
    return lax.dot_general(a, b, dims, preferred_element_type=F32)


def split(x):
    high = x.astype(BF16)
    return high, (x - high.astype(F32)).astype(BF16)


def spread(x):
    return jnp.broadcast_to(x, (SUB, LANES))


def eliminate(panel, base):
    columns = [spread(panel[:, base + j : base + j + 1]) for j in range(SUB)]
    e = [[spread(columns[j][i : i + 1, :]) for j in range(SUB)] for i in range(SUB)]
    rows = [spread(panel[i : i + 1, :]) for i in range(SUB)]
    for k in range(0, SUB, 2):
        a, b, d = e[k][k], e[k][k + 1], e[k + 1][k + 1]
        r = 1.0 / (a * d - b * b)
        first, cross, last = d * r, b * r, a * r

        def pair(x, y):
            return first * x - cross * y, last * y - cross * x

        rows[k], rows[k + 1] = pair(rows[k], rows[k + 1])
        for j in range(k + 2, SUB):
            e[k][j], e[k + 1][j] = pair(e[k][j], e[k + 1][j])
        for i in range(SUB):
            if i in (k, k + 1):
                continue
            p, q = e[i][k], e[i][k + 1]
            rows[i] = rows[i] - p * rows[k] - q * rows[k + 1]
            for j in range(k + 2, SUB):
                e[i][j] = e[i][j] - p * e[k][j] - q * e[k + 1][j]
    return rows


def solve(blocks, base):
    row_id = lax.broadcasted_iota(jnp.int32, (SUB, LANES), 0)
    blocks, n = list(blocks), len(blocks)
    for b in range(n):
        at = base + SUB * b
        rows = eliminate(blocks[b], at)
        for j in [(b + 1 + i) % n for i in range(n - 1)]:
            terms = [spread(blocks[j][:, at + k : at + k + 1]) * rows[k] for k in range(SUB)]
            while len(terms) > 1:
                terms = [x + y for x, y in zip(terms[::2], terms[1::2])]
            blocks[j] = blocks[j] - terms[0]
        panel = rows[SUB - 1]
        for k in range(SUB - 1):
            panel = jnp.where(row_id == k, rows[k], panel)
        blocks[b] = panel
    return blocks


def square(t):
    first, rest = t.astype(BF16), t - t.astype(BF16).astype(F32)
    second, third = rest.astype(BF16), (rest - rest.astype(BF16).astype(F32)).astype(BF16)
    tall = [jnp.concatenate([jnp.zeros_like(x), x], axis=0) for x in (first, second, third)]
    small = mm(first, tall[2], NT) + mm(third, tall[0], NT) + mm(second, tall[1], NT)
    return small + (mm(first, tall[1], NT) + mm(second, tall[0], NT)) + mm(first, tall[0], NT)


def mixer_of(t):
    shift = ridge_scale * (jnp.sum(t * t) / RANK + 1e-06)
    rows = lax.broadcasted_iota(jnp.int32, t.shape, 0)
    lanes = lax.broadcasted_iota(jnp.int32, t.shape, 1)
    wide = square(t) + t + jnp.where(rows + RANK == lanes, shift, 0.0)
    blocks = solve([wide[SUB * b : SUB * b + SUB] for b in range(RANK // SUB)], RANK)
    return jnp.concatenate(blocks, axis=0)


def sketch_kernel(
    nv, nf, fc, vc,
    m_hbm, vp_hbm, fp_hbm, m_buf, ft_out, w_buf,
    c_buf, vpt, fpt, f_send, f_recv, ft_full, v_send, v_recv, vt_full, t_acc, t_mine, t_recv, t_sum, t_wide, mix,
    m_sem, p_sem, f_sem, fg_sem, v_sem, vg_sem, ta_sem, tb_sem,
):
    mv, mf = lax.axis_index("vox"), lax.axis_index("frm")
    frames, voxels = m_buf.shape
    fb, vb = frames // nv, voxels // nf
    rows, columns = fb * fc, vb * vc
    row_chunks, column_chunks = nv // fc, nf // vc

    def row_chunk(s):
        return lax.rem(mv // fc + 1 + s, row_chunks)

    def rows_of(c):
        return pl.ds(pl.multiple_of(c * rows, rows), rows)

    def load(s):
        at = rows_of(row_chunk(s))
        return pltpu.make_async_copy(m_hbm.at[at], m_buf.at[at], m_sem.at[s])

    vp_load = pltpu.make_async_copy(vp_hbm, vpt, p_sem.at[0])
    fp_load = pltpu.make_async_copy(fp_hbm, fpt, p_sem.at[1])
    vp_load.start()
    load(0).start()
    fp_load.start()
    for s in range(1, row_chunks):
        load(s).start()

    barrier = pltpu.get_barrier_semaphore()
    for d in range(1, nv):
        pl.semaphore_signal(barrier, inc=1, device_id={"vox": lax.rem(mv + d, nv)}, device_id_type=MESH)
    for d in range(1, nf):
        pl.semaphore_signal(barrier, inc=1, device_id={"frm": lax.rem(mf + d, nf)}, device_id_type=MESH)

    def to(axis, src, dst, sems, it, target):
        return pltpu.make_async_remote_copy(
            src_ref=src, dst_ref=dst, send_sem=sems.at[it, 0], recv_sem=sems.at[it, 1],
            device_id={axis: target}, device_id_type=MESH,
        )

    def vox_peer(d):
        return lax.rem(mv + d, nv)

    def frm_peer(d):
        return lax.rem(mf + d, nf)

    def f_to(it, owner):
        slot = lax.rem(owner - mv + nv, nv) - 1
        return to("vox", f_send.at[it, owner], f_recv.at[it, slot], f_sem, it, owner)

    def v_to(it, owner):
        slot = lax.rem(owner - mf + nf, nf) - 1
        return to("frm", v_send.at[it, owner], v_recv.at[it, slot], v_sem, it, owner)

    def whole(kind, it):
        if kind == "f":
            return to("vox", f_recv.at[it], f_recv.at[it], f_sem, it, vox_peer(1))
        if kind == "fg":
            part = ft_full.at[it, pl.ds(0, nv - 1)]
            return to("vox", part, part, fg_sem, it, vox_peer(1))
        if kind == "v":
            return to("frm", v_recv.at[it], v_recv.at[it], v_sem, it, frm_peer(1))
        if kind == "vg":
            part = vt_full.at[it, pl.ds(0, nf - 1)]
            return to("frm", part, part, vg_sem, it, frm_peer(1))
        if kind == "ta":
            return to("frm", t_recv.at[it], t_recv.at[it], ta_sem, it, frm_peer(1))
        return to("vox", t_wide.at[it], t_wide.at[it], tb_sem, it, vox_peer(1))

    for it in range(ITERS):
        src = m_buf if it == 0 else c_buf

        def frame_step(s, carry):
            c = row_chunk(s)
            if it == 0:
                load(s).wait()
            else:
                left = jnp.concatenate([ft_full[it - 1, fc * c + i] for i in range(fc)], axis=1).T
                for j in range(voxels // WIDE):
                    at = (rows_of(c), pl.ds(j * WIDE, WIDE))
                    low = mm(left, w_buf[:, at[1]], NN)
                    floor, roof = (low - cutoff).astype(BF16), (low + cutoff).astype(BF16)
                    c_buf[at] = jnp.minimum(jnp.maximum(m_buf[at], floor), roof)
            ft = mm(vpt[...], src[rows_of(c), :], NT)
            high, low_part = split(ft)
            for i in range(fc):
                f_send[it, fc * c + i] = high[:, i * fb : (i + 1) * fb]
            probe = fpt[:, rows_of(c)]
            t_acc[...] += mm(high, probe, NT) + mm(low_part, probe, NT)
            if it > 0:
                for i in range(fc):
                    owner = fc * c + i

                    @pl.when(owner != mv)
                    def _():
                        f_to(it, owner).start()

            return carry

        t_acc[...] = jnp.zeros_like(t_acc)
        if it == 0:
            vp_load.wait()
            fp_load.wait()
        lax.fori_loop(0, row_chunks, frame_step, 0)

        t_mine[it] = jnp.concatenate([t_acc[:HALF, :], t_acc[HALF:, :]], axis=1)
        if it == 0:
            pl.semaphore_wait(barrier, nv + nf - 2)
        for d in range(1, nf):
            to("frm", t_mine.at[it], t_recv.at[it, d - 1], ta_sem, it, frm_peer(d)).start()
        if it == 0:
            for d in range(1, nv):
                f_to(it, vox_peer(d)).start()

        def voxel_step(s, carry):
            c = lax.rem(mf // vc + 1 + s, column_chunks)
            at = pl.ds(pl.multiple_of(c * columns, columns), columns)
            vt = mm(fpt[...], src[:, at], NN).astype(BF16)
            for i in range(vc):
                owner = vc * c + i
                v_send[it, owner] = vt[:, i * vb : (i + 1) * vb]

                @pl.when(owner != mf)
                def _():
                    v_to(it, owner).start()

            return carry

        lax.fori_loop(0, column_chunks, voxel_step, 0)

        whole("ta", it).wait_recv()
        part = t_mine[it]
        for d in range(nf - 1):
            part = part + t_recv[it, d]
        t_sum[it] = part
        for d in range(1, nv):
            to("vox", t_sum.at[it], t_wide.at[it, d - 1], tb_sem, it, vox_peer(d)).start()

        whole("f", it).wait_recv()
        share = f_send[it, mv].astype(F32)
        for d in range(nv - 1):
            share = share + f_recv[it, d].astype(F32)
        ft_full[it, mv] = share.astype(BF16)
        for d in range(1, nv):
            to("vox", ft_full.at[it, mv], ft_full.at[it, mv], fg_sem, it, vox_peer(d)).start()

        whole("v", it).wait_recv()
        share = v_send[it, mf].astype(F32)
        for d in range(nf - 1):
            share = share + v_recv[it, d].astype(F32)
        vt_full[it, mf] = share.astype(BF16)
        for d in range(1, nf):
            to("frm", vt_full.at[it, mf], vt_full.at[it, mf], vg_sem, it, frm_peer(d)).start()

        whole("tb", it).wait_recv()
        part = t_sum[it]
        for d in range(nv - 1):
            part = part + t_wide[it, d]
        lanes = lax.broadcasted_iota(jnp.int32, part.shape, 1)
        left_half = jnp.where(lanes < RANK, part, 0.0)
        right_half = pltpu.roll(jnp.where(lanes < RANK, 0.0, part), RANK, 1)
        mixer = mixer_of(jnp.concatenate([left_half, right_half], axis=0))
        mix[0], mix[1] = split(mixer)

        whole("vg", it).wait_recv()
        for b in range(nf):
            right = vt_full[it, b]
            w = mm(mix[0, :, :RANK], right, NN) + mm(mix[1, :, :RANK], right, NN)
            w_buf[:, b * vb : (b + 1) * vb] = w.astype(BF16)
        whole("fg", it).wait_recv()

    ft_out[...] = ft_full[ITERS - 1]
    for it in range(ITERS):
        for kind in ("f", "fg", "v", "vg", "ta", "tb"):
            whole(kind, it).wait_send()


WIDE = 512


def output_kernel(rows, m_ref, ft_ref, w_ref, low_ref, sparse_ref):
    at = pl.ds(pl.multiple_of(pl.program_id(0) * rows, rows), rows)
    left = jnp.concatenate([ft_ref[i] for i in range(ft_ref.shape[0])], axis=1).T
    for j in range(m_ref.shape[1] // WIDE):
        cols = pl.ds(j * WIDE, WIDE)
        low = mm(left, w_ref[:, cols], NN)
        rest = m_ref[at, cols].astype(F32) - low
        low_ref[:, cols] = low.astype(BF16)
        sparse_ref[:, cols] = (rest - jnp.clip(rest, -cutoff, cutoff)).astype(BF16)


def solution(mesh):
    nv, nf = mesh.shape["vox"], mesh.shape["frm"]

    def on_device(movie_matrix, voxel_probe, frame_probe):
        frames, voxels = movie_matrix.shape
        fb, vb = frames // nv, voxels // nf
        vmem = pl.BlockSpec(memory_space=pltpu.VMEM)
        hbm = pl.BlockSpec(memory_space=pltpu.HBM)
        dma = pltpu.SemaphoreType.DMA
        fc, vc = 4, 2
        movie, ft, w = pl.pallas_call(
            functools.partial(sketch_kernel, nv, nf, fc, vc),
            out_shape=(
                jax.ShapeDtypeStruct((frames, voxels), BF16),
                jax.ShapeDtypeStruct((nv, RANK, fb), BF16),
                jax.ShapeDtypeStruct((RANK, voxels), BF16),
            ),
            in_specs=[hbm, hbm, hbm],
            out_specs=(vmem, vmem, vmem),
            scratch_shapes=[
                pltpu.VMEM((frames, voxels), BF16),
                pltpu.VMEM((RANK, voxels), BF16),
                pltpu.VMEM((RANK, frames), BF16),
                pltpu.VMEM((ITERS, nv, RANK, fb), BF16),
                pltpu.VMEM((ITERS, nv - 1, RANK, fb), BF16),
                pltpu.VMEM((ITERS, nv, RANK, fb), BF16),
                pltpu.VMEM((ITERS, nf, RANK, vb), BF16),
                pltpu.VMEM((ITERS, nf - 1, RANK, vb), BF16),
                pltpu.VMEM((ITERS, nf, RANK, vb), BF16),
                pltpu.VMEM((RANK, RANK), F32),
                pltpu.VMEM((ITERS, HALF, LANES), F32),
                pltpu.VMEM((ITERS, nf - 1, HALF, LANES), F32),
                pltpu.VMEM((ITERS, HALF, LANES), F32),
                pltpu.VMEM((ITERS, nv - 1, HALF, LANES), F32),
                pltpu.VMEM((2, RANK, LANES), BF16),
                dma((nv // fc,)),
                dma((2,)),
            ]
            + [dma((ITERS, 2))] * 6,
            compiler_params=pltpu.CompilerParams(
                collective_id=0, has_side_effects=True, vmem_limit_bytes=40 * 1024 * 1024
            ),
            name="sketches",
        )(movie_matrix, voxel_probe.T, frame_probe.T)
        per = 2
        rows = per * fb
        block = pl.BlockSpec((rows, voxels), lambda i: (i, 0))
        return pl.pallas_call(
            functools.partial(output_kernel, rows),
            grid=(frames // rows,),
            out_shape=(
                jax.ShapeDtypeStruct((frames, voxels), BF16),
                jax.ShapeDtypeStruct((frames, voxels), BF16),
            ),
            in_specs=[vmem, pl.BlockSpec((per, RANK, fb), lambda i: (i, 0, 0)), vmem],
            out_specs=(block, block),
            compiler_params=pltpu.CompilerParams(vmem_limit_bytes=24 * 1024 * 1024),
            name="outputs",
        )(movie, ft, w)

    return jax.shard_map(
        on_device,
        mesh=mesh,
        in_specs=(P("frm", "vox"), P("vox", None), P("frm", None)),
        out_specs=(P("frm", "vox"), P("frm", "vox")),
        check_vma=False,
    )
```

```python
import functools

import jax
import jax.numpy as jnp
from jax import lax
from jax.experimental import pallas as pl
from jax.experimental.pallas import tpu as pltpu
from jax.sharding import PartitionSpec as P

MESH = pl.DeviceIdType.MESH
BF16, F32 = jnp.bfloat16, jnp.float32
ITERS = 2
RANK = 64
HALF = RANK // 2
WIDE = 256
SUB, LANES = 8, 128
cutoff = 1.0
ridge_scale = 0.1
NN = (((1,), (0,)), ((), ()))
NT = (((1,), (1,)), ((), ()))


def mm(a, b, dims):
    return lax.dot_general(a, b, dims, preferred_element_type=F32)


def split(x):
    high = x.astype(BF16)
    return high, (x - high.astype(F32)).astype(BF16)


def spread(x):
    return jnp.broadcast_to(x, (SUB, LANES))


def eliminate(panel, base):
    columns = [spread(panel[:, base + j : base + j + 1]) for j in range(SUB)]
    e = [[spread(columns[j][i : i + 1, :]) for j in range(SUB)] for i in range(SUB)]
    rows = [spread(panel[i : i + 1, :]) for i in range(SUB)]
    for k in range(0, SUB, 2):
        a, b, d = e[k][k], e[k][k + 1], e[k + 1][k + 1]
        r = 1.0 / (a * d - b * b)
        first, cross, last = d * r, b * r, a * r

        def pair(x, y):
            return first * x - cross * y, last * y - cross * x

        rows[k], rows[k + 1] = pair(rows[k], rows[k + 1])
        for j in range(k + 2, SUB):
            e[k][j], e[k + 1][j] = pair(e[k][j], e[k + 1][j])
        for i in range(SUB):
            if i in (k, k + 1):
                continue
            p, q = e[i][k], e[i][k + 1]
            rows[i] = rows[i] - p * rows[k] - q * rows[k + 1]
            for j in range(k + 2, SUB):
                e[i][j] = e[i][j] - p * e[k][j] - q * e[k + 1][j]
    return rows


def solve(blocks, base):
    row_id = lax.broadcasted_iota(jnp.int32, (SUB, LANES), 0)
    blocks, n = list(blocks), len(blocks)
    for b in range(n):
        at = base + SUB * b
        rows = eliminate(blocks[b], at)
        for j in [(b + 1 + i) % n for i in range(n - 1)]:
            terms = [spread(blocks[j][:, at + k : at + k + 1]) * rows[k] for k in range(SUB)]
            while len(terms) > 1:
                terms = [x + y for x, y in zip(terms[::2], terms[1::2])]
            blocks[j] = blocks[j] - terms[0]
        panel = rows[SUB - 1]
        for k in range(SUB - 1):
            panel = jnp.where(row_id == k, rows[k], panel)
        blocks[b] = panel
    return blocks


def square(t):
    first, rest = t.astype(BF16), t - t.astype(BF16).astype(F32)
    second, third = rest.astype(BF16), (rest - rest.astype(BF16).astype(F32)).astype(BF16)
    tall = [jnp.concatenate([jnp.zeros_like(x), x], axis=0) for x in (first, second, third)]
    small = mm(first, tall[2], NT) + mm(third, tall[0], NT) + mm(second, tall[1], NT)
    return small + (mm(first, tall[1], NT) + mm(second, tall[0], NT)) + mm(first, tall[0], NT)


def mixer_of(t):
    shift = ridge_scale * (jnp.sum(t * t) / RANK + 1e-06)
    rows = lax.broadcasted_iota(jnp.int32, t.shape, 0)
    lanes = lax.broadcasted_iota(jnp.int32, t.shape, 1)
    wide = square(t) + t + jnp.where(rows + RANK == lanes, shift, 0.0)
    blocks = solve([wide[SUB * b : SUB * b + SUB] for b in range(RANK // SUB)], RANK)
    return jnp.concatenate(blocks, axis=0)


def far_first(n, inner):
    def hops(d):
        outer = n // inner
        return min(d // inner, outer - d // inner) + min(d % inner, inner - d % inner)

    return sorted(range(1, n), key=lambda d: -hops(d))


def sketch_kernel(
    nv, nf, side, cores, fc, vc,
    m_hbm, vp_hbm, fp_hbm, m_buf, ft_out, w_buf,
    c_buf, vpt, fpt, f_send, f_recv, ft_full, v_send, v_recv, vt_full, t_acc, t_mine, t_recv, t_sum, t_wide, mix,
    m_sem, p_sem, f_sem, fg_sem, v_sem, vg_sem, ta_sem, tb_sem,
):
    mv, mf = lax.axis_index("vox"), lax.axis_index("frm")
    frames, voxels = m_buf.shape
    fb, vb = frames // nv, voxels // nf
    rows, columns = fb * fc, vb * vc
    row_chunks, column_chunks = nv // fc, nf // vc

    def row_chunk(s):
        return lax.rem(mv // fc + 1 + s, row_chunks)

    def rows_of(c):
        return pl.ds(pl.multiple_of(c * rows, rows), rows)

    def load(s):
        at = rows_of(row_chunk(s))
        return pltpu.make_async_copy(m_hbm.at[at], m_buf.at[at], m_sem.at[s])

    vp_load = pltpu.make_async_copy(vp_hbm, vpt, p_sem.at[0])
    fp_load = pltpu.make_async_copy(fp_hbm, fpt, p_sem.at[1])
    vp_load.start()
    load(0).start()
    fp_load.start()
    for s in range(1, row_chunks):
        load(s).start()

    def vox_peer(d):
        return (mv // side + d // side) % (nv // side) * side + (mv + d) % side

    def frm_peer(d):
        return (mf // cores + d // cores) % (nf // cores) * cores + (mf + d) % cores

    vox_order, frm_order = far_first(nv, side), far_first(nf, cores)
    barrier = pltpu.get_barrier_semaphore()
    for d in vox_order:
        pl.semaphore_signal(barrier, inc=1, device_id={"vox": vox_peer(d)}, device_id_type=MESH)
    for d in frm_order:
        pl.semaphore_signal(barrier, inc=1, device_id={"frm": frm_peer(d)}, device_id_type=MESH)

    def to(axis, src, dst, sems, it, target):
        return pltpu.make_async_remote_copy(
            src_ref=src, dst_ref=dst, send_sem=sems.at[it, 0], recv_sem=sems.at[it, 1],
            device_id={axis: target}, device_id_type=MESH,
        )

    def f_to(it, owner):
        slot = (owner // side - mv // side + nv // side) % (nv // side) * side + (owner - mv + nv) % side - 1
        return to("vox", f_send.at[it, owner], f_recv.at[it, slot], f_sem, it, owner)

    def v_to(it, owner):
        slot = (owner // cores - mf // cores + nf // cores) % (nf // cores) * cores + (owner - mf + nf) % cores - 1
        return to("frm", v_send.at[it, owner], v_recv.at[it, slot], v_sem, it, owner)

    def whole(kind, it):
        if kind == "f":
            return to("vox", f_recv.at[it], f_recv.at[it], f_sem, it, vox_peer(1))
        if kind == "fg":
            part = ft_full.at[it, pl.ds(0, nv - 1)]
            return to("vox", part, part, fg_sem, it, vox_peer(1))
        if kind == "v":
            return to("frm", v_recv.at[it], v_recv.at[it], v_sem, it, frm_peer(1))
        if kind == "vg":
            part = vt_full.at[it, pl.ds(0, nf - 1)]
            return to("frm", part, part, vg_sem, it, frm_peer(1))
        if kind == "ta":
            return to("frm", t_recv.at[it], t_recv.at[it], ta_sem, it, frm_peer(1))
        return to("vox", t_wide.at[it], t_wide.at[it], tb_sem, it, vox_peer(1))

    for it in range(ITERS):
        src = m_buf if it == 0 else c_buf

        def frame_step(s, carry):
            c = row_chunk(s)
            if it == 0:
                load(s).wait()
            else:
                left = jnp.concatenate([ft_full[it - 1, fc * c + i] for i in range(fc)], axis=1).T
                for j in range(voxels // WIDE):
                    at = (rows_of(c), pl.ds(j * WIDE, WIDE))
                    low = mm(left, w_buf[:, at[1]], NN)
                    floor, roof = (low - cutoff).astype(BF16), (low + cutoff).astype(BF16)
                    c_buf[at] = jnp.minimum(jnp.maximum(m_buf[at], floor), roof)
            ft = mm(vpt[...], src[rows_of(c), :], NT)
            high, low_part = split(ft)
            for i in range(fc):
                f_send[it, fc * c + i] = high[:, i * fb : (i + 1) * fb]
            probe = fpt[:, rows_of(c)]
            t_acc[...] += mm(high, probe, NT) + mm(low_part, probe, NT)
            if it > 0:
                for i in range(fc):
                    owner = fc * c + i

                    @pl.when(owner != mv)
                    def _():
                        f_to(it, owner).start()

            return carry

        t_acc[...] = jnp.zeros_like(t_acc)
        if it == 0:
            vp_load.wait()
            fp_load.wait()
        lax.fori_loop(0, row_chunks, frame_step, 0)

        t_mine[it] = jnp.concatenate([t_acc[:HALF, :], t_acc[HALF:, :]], axis=1)
        if it == 0:
            pl.semaphore_wait(barrier, nv + nf - 2)
        for d in frm_order:
            to("frm", t_mine.at[it], t_recv.at[it, d - 1], ta_sem, it, frm_peer(d)).start()
        if it == 0:
            for d in vox_order:
                f_to(it, vox_peer(d)).start()

        def voxel_step(s, carry):
            c = lax.rem(mf // vc + 1 + s, column_chunks)
            at = pl.ds(pl.multiple_of(c * columns, columns), columns)
            vt = mm(fpt[...], src[:, at], NN).astype(BF16)
            for i in range(vc):
                owner = vc * c + i
                v_send[it, owner] = vt[:, i * vb : (i + 1) * vb]

                @pl.when(owner != mf)
                def _():
                    v_to(it, owner).start()

            return carry

        lax.fori_loop(0, column_chunks, voxel_step, 0)

        whole("ta", it).wait_recv()
        part = t_mine[it]
        for d in range(nf - 1):
            part = part + t_recv[it, d]
        t_sum[it] = part
        for d in vox_order:
            to("vox", t_sum.at[it], t_wide.at[it, d - 1], tb_sem, it, vox_peer(d)).start()

        whole("f", it).wait_recv()
        share = f_send[it, mv].astype(F32)
        for d in range(nv - 1):
            share = share + f_recv[it, d].astype(F32)
        ft_full[it, mv] = share.astype(BF16)
        for d in vox_order:
            to("vox", ft_full.at[it, mv], ft_full.at[it, mv], fg_sem, it, vox_peer(d)).start()

        whole("v", it).wait_recv()
        share = v_send[it, mf].astype(F32)
        for d in range(nf - 1):
            share = share + v_recv[it, d].astype(F32)
        vt_full[it, mf] = share.astype(BF16)
        for d in frm_order:
            to("frm", vt_full.at[it, mf], vt_full.at[it, mf], vg_sem, it, frm_peer(d)).start()

        whole("tb", it).wait_recv()
        part = t_sum[it]
        for d in range(nv - 1):
            part = part + t_wide[it, d]
        lanes = lax.broadcasted_iota(jnp.int32, part.shape, 1)
        left_half = jnp.where(lanes < RANK, part, 0.0)
        right_half = pltpu.roll(jnp.where(lanes < RANK, 0.0, part), RANK, 1)
        mixer = mixer_of(jnp.concatenate([left_half, right_half], axis=0))
        mix[0], mix[1] = split(mixer)

        whole("vg", it).wait_recv()
        for b in range(nf):
            right = vt_full[it, b]
            w = mm(mix[0, :, :RANK], right, NN) + mm(mix[1, :, :RANK], right, NN)
            w_buf[:, b * vb : (b + 1) * vb] = w.astype(BF16)
        whole("fg", it).wait_recv()

    ft_out[...] = ft_full[ITERS - 1]
    for it in range(ITERS):
        for kind in ("f", "fg", "v", "vg", "ta", "tb"):
            whole(kind, it).wait_send()


def output_kernel(per, m_ref, ft_ref, w_ref, low_hbm, sparse_hbm, low_buf, sparse_buf, sems):
    slots, rows, voxels = low_buf.shape
    steps = ft_ref.shape[0] // per

    def copies(i):
        at, k = pl.ds(i * rows, rows), i % slots
        return (
            pltpu.make_async_copy(low_buf.at[k], low_hbm.at[at], sems.at[0, k]),
            pltpu.make_async_copy(sparse_buf.at[k], sparse_hbm.at[at], sems.at[1, k]),
        )

    for i in range(steps):
        k = i % slots
        if i >= slots:
            for copy in copies(i - slots):
                copy.wait()
        left = jnp.concatenate([ft_ref[per * i + q] for q in range(per)], axis=1).T
        for j in range(voxels // WIDE):
            cols = pl.ds(j * WIDE, WIDE)
            low = mm(left, w_ref[:, cols], NN)
            rest = m_ref[pl.ds(i * rows, rows), cols].astype(F32) - low
            low_buf[k, :, cols] = low.astype(BF16)
            sparse_buf[k, :, cols] = (rest - jnp.clip(rest, -cutoff, cutoff)).astype(BF16)
        for copy in copies(i):
            copy.start()
    for i in range(steps - slots, steps):
        for copy in copies(i):
            copy.wait()


def solution(mesh):
    nv, nf = mesh.shape["vox"], mesh.shape["frm"]

    def on_device(movie_matrix, voxel_probe, frame_probe):
        frames, voxels = movie_matrix.shape
        fb, vb = frames // nv, voxels // nf
        vmem = pl.BlockSpec(memory_space=pltpu.VMEM)
        hbm = pl.BlockSpec(memory_space=pltpu.HBM)
        dma = pltpu.SemaphoreType.DMA
        fc, vc = nv // 2, nf // 2
        movie, ft, w = pl.pallas_call(
            functools.partial(sketch_kernel, nv, nf, 4, 2, fc, vc),
            out_shape=(
                jax.ShapeDtypeStruct((frames, voxels), BF16),
                jax.ShapeDtypeStruct((nv, RANK, fb), BF16),
                jax.ShapeDtypeStruct((RANK, voxels), BF16),
            ),
            in_specs=[hbm, hbm, hbm],
            out_specs=(vmem, vmem, vmem),
            scratch_shapes=[
                pltpu.VMEM((frames, voxels), BF16),
                pltpu.VMEM((RANK, voxels), BF16),
                pltpu.VMEM((RANK, frames), BF16),
                pltpu.VMEM((ITERS, nv, RANK, fb), BF16),
                pltpu.VMEM((ITERS, nv - 1, RANK, fb), BF16),
                pltpu.VMEM((ITERS, nv, RANK, fb), BF16),
                pltpu.VMEM((ITERS, nf, RANK, vb), BF16),
                pltpu.VMEM((ITERS, nf - 1, RANK, vb), BF16),
                pltpu.VMEM((ITERS, nf, RANK, vb), BF16),
                pltpu.VMEM((RANK, RANK), F32),
                pltpu.VMEM((ITERS, HALF, LANES), F32),
                pltpu.VMEM((ITERS, nf - 1, HALF, LANES), F32),
                pltpu.VMEM((ITERS, HALF, LANES), F32),
                pltpu.VMEM((ITERS, nv - 1, HALF, LANES), F32),
                pltpu.VMEM((2, RANK, LANES), BF16),
                dma((nv // fc,)),
                dma((2,)),
            ]
            + [dma((ITERS, 2))] * 6,
            compiler_params=pltpu.CompilerParams(
                collective_id=0, has_side_effects=True, vmem_limit_bytes=40 * 1024 * 1024
            ),
            name="sketches",
        )(
            movie_matrix,
            pltpu.with_memory_space_constraint(voxel_probe.T, pltpu.HBM),
            pltpu.with_memory_space_constraint(frame_probe.T, pltpu.HBM),
        )
        per, slots = 2, 4
        return pl.pallas_call(
            functools.partial(output_kernel, per),
            out_shape=(
                jax.ShapeDtypeStruct((frames, voxels), BF16),
                jax.ShapeDtypeStruct((frames, voxels), BF16),
            ),
            in_specs=[vmem, vmem, vmem],
            out_specs=(hbm, hbm),
            scratch_shapes=[pltpu.VMEM((slots, per * fb, voxels), BF16)] * 2 + [dma((2, slots))],
            compiler_params=pltpu.CompilerParams(vmem_limit_bytes=24 * 1024 * 1024),
            name="outputs",
        )(movie, ft, w)

    return jax.shard_map(
        on_device,
        mesh=mesh,
        in_specs=(P("frm", "vox"), P("vox", None), P("frm", None)),
        out_specs=(P("frm", "vox"), P("frm", "vox")),
        check_vma=False,
    )
```

```python
import functools

import jax
import jax.numpy as jnp
from jax import lax
from jax.experimental import pallas as pl
from jax.experimental.pallas import tpu as pltpu
from jax.sharding import PartitionSpec as P

MESH = pl.DeviceIdType.MESH
BF16, F32 = jnp.bfloat16, jnp.float32
ITERS = 2
RANK = 64
HALF = RANK // 2
WIDE = 256
SUB, LANES = 8, 128
cutoff = 1.0
ridge_scale = 0.1
NN = (((1,), (0,)), ((), ()))
NT = (((1,), (1,)), ((), ()))


def mm(a, b, dims):
    return lax.dot_general(a, b, dims, preferred_element_type=F32)


def split(x):
    high = x.astype(BF16)
    return high, (x - high.astype(F32)).astype(BF16)


def spread(x):
    return jnp.broadcast_to(x, (SUB, LANES))


def eliminate(panel, base, keep):
    for j in range(SUB):
        keep[j] = spread(panel[:, base + j : base + j + 1])
    upper = {(i, j): spread(keep[j, i : i + 1, :]) for j in range(SUB) for i in range(j + 1)}
    e = [[upper[min(i, j), max(i, j)] for j in range(SUB)] for i in range(SUB)]
    rows = [spread(panel[i : i + 1, :]) for i in range(SUB)]
    for k in range(0, SUB, 2):
        a, b, d = e[k][k], e[k][k + 1], e[k + 1][k + 1]
        r = 1.0 / (a * d - b * b)
        first, cross, last = d * r, b * r, a * r

        def pair(x, y):
            return first * x - cross * y, last * y - cross * x

        rows[k], rows[k + 1] = pair(rows[k], rows[k + 1])
        for j in range(k + 2, SUB):
            e[k][j], e[k + 1][j] = pair(e[k][j], e[k + 1][j])
        for i in range(SUB):
            if i in (k, k + 1):
                continue
            p, q = e[i][k], e[i][k + 1]
            rows[i] = rows[i] - p * rows[k] - q * rows[k + 1]
            for j in range(k + 2, SUB):
                e[i][j] = e[i][j] - p * e[k][j] - q * e[k + 1][j]
    return rows


def solve(blocks, base, keep):
    row_id = lax.broadcasted_iota(jnp.int32, (SUB, LANES), 0)
    blocks, n = list(blocks), len(blocks)
    for b in range(n):
        at = base + SUB * b
        rows = eliminate(blocks[b], at, keep.at[b])
        for j in [(b + 1 + i) % n for i in range(n - 1)]:
            terms = [spread(blocks[j][:, at + k : at + k + 1]) * rows[k] for k in range(SUB)]
            while len(terms) > 1:
                terms = [x + y for x, y in zip(terms[::2], terms[1::2])]
            blocks[j] = blocks[j] - terms[0]
        panel = rows[SUB - 1]
        for k in range(SUB - 1):
            panel = jnp.where(row_id == k, rows[k], panel)
        blocks[b] = panel
    return blocks


def square(t):
    first, rest = t.astype(BF16), t - t.astype(BF16).astype(F32)
    second, third = rest.astype(BF16), (rest - rest.astype(BF16).astype(F32)).astype(BF16)
    tall = [jnp.concatenate([jnp.zeros_like(x), x], axis=0) for x in (first, second, third)]
    small = mm(first, tall[2], NT) + mm(third, tall[0], NT) + mm(second, tall[1], NT)
    return small + (mm(first, tall[1], NT) + mm(second, tall[0], NT)) + mm(first, tall[0], NT)


def mixer_of(t, keep):
    shift = ridge_scale * (jnp.sum(t * t) / RANK + 1e-06)
    rows = lax.broadcasted_iota(jnp.int32, t.shape, 0)
    lanes = lax.broadcasted_iota(jnp.int32, t.shape, 1)
    wide = square(t) + t + jnp.where(rows + RANK == lanes, shift, 0.0)
    blocks = solve([wide[SUB * b : SUB * b + SUB] for b in range(RANK // SUB)], RANK, keep)
    return jnp.concatenate(blocks, axis=0)


def far_first(n, inner):
    def hops(d):
        outer = n // inner
        return min(d // inner, outer - d // inner) + min(d % inner, inner - d % inner)

    return sorted(range(1, n), key=lambda d: -hops(d))


def sketch_kernel(
    nv, nf, side, cores, fc, vc,
    m_hbm, vp_hbm, fp_hbm, m_buf, ft_out, w_buf,
    c_buf, vpt, fpt, f_send, f_recv, ft_full, v_send, v_recv, vt_full, t_acc, t_mine, t_recv, t_sum, t_wide, mix, keep,
    m_sem, p_sem, f_sem, fg_sem, v_sem, vg_sem, ta_sem, tb_sem,
):
    mv, mf = lax.axis_index("vox"), lax.axis_index("frm")
    frames, voxels = m_buf.shape
    fb, vb = frames // nv, voxels // nf
    rows, columns = fb * fc, vb * vc
    row_chunks, column_chunks = nv // fc, nf // vc

    def row_chunk(s):
        return lax.rem(mv // fc + 1 + s, row_chunks)

    def rows_of(c):
        return pl.ds(pl.multiple_of(c * rows, rows), rows)

    def load(s):
        at = rows_of(row_chunk(s))
        return pltpu.make_async_copy(m_hbm.at[at], m_buf.at[at], m_sem.at[s])

    vp_load = pltpu.make_async_copy(vp_hbm, vpt, p_sem.at[0])
    fp_load = pltpu.make_async_copy(fp_hbm, fpt, p_sem.at[1])
    vp_load.start()
    load(0).start()
    fp_load.start()
    for s in range(1, row_chunks):
        load(s).start()

    def vox_peer(d):
        return (mv // side + d // side) % (nv // side) * side + (mv + d) % side

    def frm_peer(d):
        return (mf // cores + d // cores) % (nf // cores) * cores + (mf + d) % cores

    vox_order, frm_order = far_first(nv, side), far_first(nf, cores)
    barrier = pltpu.get_barrier_semaphore()
    for d in vox_order:
        pl.semaphore_signal(barrier, inc=1, device_id={"vox": vox_peer(d)}, device_id_type=MESH)
    for d in frm_order:
        pl.semaphore_signal(barrier, inc=1, device_id={"frm": frm_peer(d)}, device_id_type=MESH)

    def to(axis, src, dst, sems, it, target):
        return pltpu.make_async_remote_copy(
            src_ref=src, dst_ref=dst, send_sem=sems.at[it, 0], recv_sem=sems.at[it, 1],
            device_id={axis: target}, device_id_type=MESH,
        )

    def f_to(it, owner):
        slot = (owner // side - mv // side + nv // side) % (nv // side) * side + (owner - mv + nv) % side - 1
        return to("vox", f_send.at[it, owner], f_recv.at[it, slot], f_sem, it, owner)

    def v_to(it, owner):
        slot = (owner // cores - mf // cores + nf // cores) % (nf // cores) * cores + (owner - mf + nf) % cores - 1
        return to("frm", v_send.at[it, owner], v_recv.at[it, slot], v_sem, it, owner)

    def whole(kind, it):
        if kind == "f":
            return to("vox", f_recv.at[it], f_recv.at[it], f_sem, it, vox_peer(1))
        if kind == "fg":
            part = ft_full.at[it, pl.ds(0, nv - 1)]
            return to("vox", part, part, fg_sem, it, vox_peer(1))
        if kind == "v":
            return to("frm", v_recv.at[it], v_recv.at[it], v_sem, it, frm_peer(1))
        if kind == "vg":
            part = vt_full.at[it, pl.ds(0, nf - 1)]
            return to("frm", part, part, vg_sem, it, frm_peer(1))
        if kind == "ta":
            return to("frm", t_recv.at[it], t_recv.at[it], ta_sem, it, frm_peer(1))
        return to("vox", t_wide.at[it], t_wide.at[it], tb_sem, it, vox_peer(1))

    for it in range(ITERS):
        src = m_buf if it == 0 else c_buf

        def frame_step(s, carry):
            c = row_chunk(s)
            if it == 0:
                load(s).wait()
            else:
                left = jnp.concatenate([ft_full[it - 1, fc * c + i] for i in range(fc)], axis=1).T
                for j in range(voxels // WIDE):
                    at = (rows_of(c), pl.ds(j * WIDE, WIDE))
                    low = mm(left, w_buf[:, at[1]], NN)
                    floor, roof = (low - cutoff).astype(BF16), (low + cutoff).astype(BF16)
                    c_buf[at] = jnp.minimum(jnp.maximum(m_buf[at], floor), roof)
            ft = mm(vpt[...], src[rows_of(c), :], NT)
            high, low_part = split(ft)
            for i in range(fc):
                f_send[it, fc * c + i] = high[:, i * fb : (i + 1) * fb]
            probe = fpt[:, rows_of(c)]
            t_acc[...] += mm(high, probe, NT) + mm(low_part, probe, NT)
            if it > 0:
                for i in range(fc):
                    owner = fc * c + i

                    @pl.when(owner != mv)
                    def _():
                        f_to(it, owner).start()

            return carry

        t_acc[...] = jnp.zeros_like(t_acc)
        if it == 0:
            vp_load.wait()
            fp_load.wait()
        lax.fori_loop(0, row_chunks, frame_step, 0)

        t_mine[it] = jnp.concatenate([t_acc[:HALF, :], t_acc[HALF:, :]], axis=1)
        if it == 0:
            pl.semaphore_wait(barrier, nv + nf - 2)
        for d in frm_order:
            to("frm", t_mine.at[it], t_recv.at[it, d - 1], ta_sem, it, frm_peer(d)).start()
        if it == 0:
            for d in vox_order:
                f_to(it, vox_peer(d)).start()

        def voxel_step(s, carry):
            c = lax.rem(mf // vc + 1 + s, column_chunks)
            at = pl.ds(pl.multiple_of(c * columns, columns), columns)
            vt = mm(fpt[...], src[:, at], NN).astype(BF16)
            for i in range(vc):
                owner = vc * c + i
                v_send[it, owner] = vt[:, i * vb : (i + 1) * vb]

                @pl.when(owner != mf)
                def _():
                    v_to(it, owner).start()

            return carry

        lax.fori_loop(0, column_chunks, voxel_step, 0)

        whole("ta", it).wait_recv()
        part = t_mine[it]
        for d in range(nf - 1):
            part = part + t_recv[it, d]
        t_sum[it] = part
        for d in vox_order:
            to("vox", t_sum.at[it], t_wide.at[it, d - 1], tb_sem, it, vox_peer(d)).start()

        whole("f", it).wait_recv()
        share = f_send[it, mv].astype(F32)
        for d in range(nv - 1):
            share = share + f_recv[it, d].astype(F32)
        ft_full[it, mv] = share.astype(BF16)
        for d in vox_order:
            to("vox", ft_full.at[it, mv], ft_full.at[it, mv], fg_sem, it, vox_peer(d)).start()

        whole("v", it).wait_recv()
        share = v_send[it, mf].astype(F32)
        for d in range(nf - 1):
            share = share + v_recv[it, d].astype(F32)
        vt_full[it, mf] = share.astype(BF16)
        for d in frm_order:
            to("frm", vt_full.at[it, mf], vt_full.at[it, mf], vg_sem, it, frm_peer(d)).start()

        whole("tb", it).wait_recv()
        part = t_sum[it]
        for d in range(nv - 1):
            part = part + t_wide[it, d]
        lanes = lax.broadcasted_iota(jnp.int32, part.shape, 1)
        left_half = jnp.where(lanes < RANK, part, 0.0)
        right_half = pltpu.roll(jnp.where(lanes < RANK, 0.0, part), RANK, 1)
        mixer = mixer_of(jnp.concatenate([left_half, right_half], axis=0), keep)
        high, low_part = split(mixer)
        both = jnp.where(lax.broadcasted_iota(jnp.int32, mixer.shape, 1) < RANK, high.astype(F32), pltpu.roll(low_part.astype(F32), RANK, 1))
        mix[...] = both.astype(BF16)

        whole("vg", it).wait_recv()
        for b in range(nf):
            right = vt_full[it, b]
            w = mm(mix[...], jnp.concatenate([right, right], axis=0), NN)
            w_buf[:, b * vb : (b + 1) * vb] = w.astype(BF16)
        whole("fg", it).wait_recv()

    ft_out[...] = ft_full[ITERS - 1]
    for it in range(ITERS):
        for kind in ("f", "fg", "v", "vg", "ta", "tb"):
            whole(kind, it).wait_send()


def output_kernel(per, m_ref, ft_ref, w_ref, low_hbm, sparse_hbm, low_buf, sparse_buf, sems):
    slots, rows, voxels = low_buf.shape
    steps = ft_ref.shape[0] // per

    def copies(i):
        at, k = pl.ds(i * rows, rows), i % slots
        return (
            pltpu.make_async_copy(low_buf.at[k], low_hbm.at[at], sems.at[0, k]),
            pltpu.make_async_copy(sparse_buf.at[k], sparse_hbm.at[at], sems.at[1, k]),
        )

    for i in range(steps):
        k = i % slots
        if i >= slots:
            for copy in copies(i - slots):
                copy.wait()
        left = jnp.concatenate([ft_ref[per * i + q] for q in range(per)], axis=1).T
        for j in range(voxels // WIDE):
            cols = pl.ds(j * WIDE, WIDE)
            low = mm(left, w_ref[:, cols], NN)
            rest = m_ref[pl.ds(i * rows, rows), cols].astype(F32) - low
            low_buf[k, :, cols] = low.astype(BF16)
            sparse_buf[k, :, cols] = (rest - jnp.clip(rest, -cutoff, cutoff)).astype(BF16)
        for copy in copies(i):
            copy.start()
    for i in range(steps - slots, steps):
        for copy in copies(i):
            copy.wait()


def solution(mesh):
    nv, nf = mesh.shape["vox"], mesh.shape["frm"]

    def on_device(movie_matrix, voxel_probe, frame_probe):
        frames, voxels = movie_matrix.shape
        fb, vb = frames // nv, voxels // nf
        vmem = pl.BlockSpec(memory_space=pltpu.VMEM)
        hbm = pl.BlockSpec(memory_space=pltpu.HBM)
        dma = pltpu.SemaphoreType.DMA
        fc, vc = nv // 2, nf // 2
        movie, ft, w = pl.pallas_call(
            functools.partial(sketch_kernel, nv, nf, 4, 2, fc, vc),
            out_shape=(
                jax.ShapeDtypeStruct((frames, voxels), BF16),
                jax.ShapeDtypeStruct((nv, RANK, fb), BF16),
                jax.ShapeDtypeStruct((RANK, voxels), BF16),
            ),
            in_specs=[hbm, hbm, hbm],
            out_specs=(vmem, vmem, vmem),
            scratch_shapes=[
                pltpu.VMEM((frames, voxels), BF16),
                pltpu.VMEM((RANK, voxels), BF16),
                pltpu.VMEM((RANK, frames), BF16),
                pltpu.VMEM((ITERS, nv, RANK, fb), BF16),
                pltpu.VMEM((ITERS, nv - 1, RANK, fb), BF16),
                pltpu.VMEM((ITERS, nv, RANK, fb), BF16),
                pltpu.VMEM((ITERS, nf, RANK, vb), BF16),
                pltpu.VMEM((ITERS, nf - 1, RANK, vb), BF16),
                pltpu.VMEM((ITERS, nf, RANK, vb), BF16),
                pltpu.VMEM((RANK, RANK), F32),
                pltpu.VMEM((ITERS, HALF, LANES), F32),
                pltpu.VMEM((ITERS, nf - 1, HALF, LANES), F32),
                pltpu.VMEM((ITERS, HALF, LANES), F32),
                pltpu.VMEM((ITERS, nv - 1, HALF, LANES), F32),
                pltpu.VMEM((RANK, LANES), BF16),
                pltpu.VMEM((RANK // SUB, SUB, SUB, LANES), F32),
                dma((nv // fc,)),
                dma((2,)),
            ]
            + [dma((ITERS, 2))] * 6,
            compiler_params=pltpu.CompilerParams(
                collective_id=0, has_side_effects=True, vmem_limit_bytes=40 * 1024 * 1024
            ),
            name="sketches",
        )(
            movie_matrix,
            pltpu.with_memory_space_constraint(voxel_probe.T, pltpu.HBM),
            pltpu.with_memory_space_constraint(frame_probe.T, pltpu.HBM),
        )
        per, slots = 2, 4
        return pl.pallas_call(
            functools.partial(output_kernel, per),
            out_shape=(
                jax.ShapeDtypeStruct((frames, voxels), BF16),
                jax.ShapeDtypeStruct((frames, voxels), BF16),
            ),
            in_specs=[vmem, vmem, vmem],
            out_specs=(hbm, hbm),
            scratch_shapes=[pltpu.VMEM((slots, per * fb, voxels), BF16)] * 2 + [dma((2, slots))],
            compiler_params=pltpu.CompilerParams(vmem_limit_bytes=24 * 1024 * 1024),
            name="outputs",
        )(movie, ft, w)

    return jax.shard_map(
        on_device,
        mesh=mesh,
        in_specs=(P("frm", "vox"), P("vox", None), P("frm", None)),
        out_specs=(P("frm", "vox"), P("frm", "vox")),
        check_vma=False,
    )
```

```python
import functools

import jax
import jax.numpy as jnp
from jax import lax
from jax.experimental import pallas as pl
from jax.experimental.pallas import tpu as pltpu
from jax.sharding import PartitionSpec as P

MESH = pl.DeviceIdType.MESH
BF16, F32 = jnp.bfloat16, jnp.float32
ITERS = 2
RANK = 64
HALF = RANK // 2
WIDE = 256
SUB, LANES = 8, 128
cutoff = 1.0
ridge_scale = 0.1
NN = (((1,), (0,)), ((), ()))
NT = (((1,), (1,)), ((), ()))


def mm(a, b, dims):
    return lax.dot_general(a, b, dims, preferred_element_type=F32)


def split(x):
    high = x.astype(BF16)
    return high, (x - high.astype(F32)).astype(BF16)


def spread(x):
    return jnp.broadcast_to(x, (SUB, LANES))


def eliminate(panel, base, keep):
    for j in range(SUB):
        keep[j] = spread(panel[:, base + j : base + j + 1])
    upper = {(i, j): spread(keep[j, i : i + 1, :]) for j in range(SUB) for i in range(j + 1)}
    e = [[upper[min(i, j), max(i, j)] for j in range(SUB)] for i in range(SUB)]
    rows = [spread(panel[i : i + 1, :]) for i in range(SUB)]
    for k in range(0, SUB, 2):
        a, b, d = e[k][k], e[k][k + 1], e[k + 1][k + 1]
        r = 1.0 / (a * d - b * b)
        first, cross, last = d * r, b * r, a * r

        def pair(x, y):
            return first * x - cross * y, last * y - cross * x

        rows[k], rows[k + 1] = pair(rows[k], rows[k + 1])
        for j in range(k + 2, SUB):
            e[k][j], e[k + 1][j] = pair(e[k][j], e[k + 1][j])
        for i in range(SUB):
            if i in (k, k + 1):
                continue
            p, q = e[i][k], e[i][k + 1]
            rows[i] = rows[i] - p * rows[k] - q * rows[k + 1]
            for j in range(k + 2, SUB):
                e[i][j] = e[i][j] - p * e[k][j] - q * e[k + 1][j]
    return rows


def solve(blocks, base, keep):
    row_id = lax.broadcasted_iota(jnp.int32, (SUB, LANES), 0)
    blocks, n = list(blocks), len(blocks)
    for b in range(n):
        at = base + SUB * b
        rows = eliminate(blocks[b], at, keep.at[b])
        for j in [(b + 1 + i) % n for i in range(n - 1)]:
            terms = [spread(blocks[j][:, at + k : at + k + 1]) * rows[k] for k in range(SUB)]
            while len(terms) > 1:
                terms = [x + y for x, y in zip(terms[::2], terms[1::2])]
            blocks[j] = blocks[j] - terms[0]
        panel = rows[SUB - 1]
        for k in range(SUB - 1):
            panel = jnp.where(row_id == k, rows[k], panel)
        blocks[b] = panel
    return blocks


def square(t):
    first, rest = t.astype(BF16), t - t.astype(BF16).astype(F32)
    second, third = rest.astype(BF16), (rest - rest.astype(BF16).astype(F32)).astype(BF16)
    tall = [jnp.concatenate([jnp.zeros_like(x), x], axis=0) for x in (first, second, third)]
    small = mm(first, tall[2], NT) + mm(third, tall[0], NT) + mm(second, tall[1], NT)
    return small + (mm(first, tall[1], NT) + mm(second, tall[0], NT)) + mm(first, tall[0], NT)


def mixer_of(t, keep):
    shift = ridge_scale * (jnp.sum(t * t) / RANK + 1e-06)
    rows = lax.broadcasted_iota(jnp.int32, t.shape, 0)
    lanes = lax.broadcasted_iota(jnp.int32, t.shape, 1)
    wide = square(t) + t + jnp.where(rows + RANK == lanes, shift, 0.0)
    blocks = solve([wide[SUB * b : SUB * b + SUB] for b in range(RANK // SUB)], RANK, keep)
    return jnp.concatenate(blocks, axis=0)


def far_first(n, inner):
    def hops(d):
        outer = n // inner
        return min(d // inner, outer - d // inner) + min(d % inner, inner - d % inner)

    return sorted(range(1, n), key=lambda d: -hops(d))


def sketch_kernel(
    nv, nf, side, cores, fc_first, vc,
    m_hbm, vp_hbm, fp_hbm, m_buf, ft_out, w_buf,
    c_buf, vpt, fpt, f_send, f_recv, ft_full, v_send, v_recv, vt_full, t_acc, t_mine, t_recv, t_sum, t_wide, mix, keep,
    m_sem, p_sem, f_sem, fg_sem, v_sem, vg_sem, ta_sem, tb_sem,
):
    mv, mf = lax.axis_index("vox"), lax.axis_index("frm")
    frames, voxels = m_buf.shape
    fb, vb = frames // nv, voxels // nf
    fc = fc_first
    columns, column_chunks = vb * vc, nf // vc
    rows, row_chunks = fb * fc, nv // fc

    def row_chunk(s, fc=fc):
        return lax.rem(mv // fc + 1 + s, nv // fc)

    def rows_of(c, rows=rows):
        return pl.ds(pl.multiple_of(c * rows, rows), rows)

    def load(s):
        at = rows_of(row_chunk(s))
        return pltpu.make_async_copy(m_hbm.at[at], m_buf.at[at], m_sem.at[s])

    vp_load = pltpu.make_async_copy(vp_hbm, vpt, p_sem.at[0])
    fp_load = pltpu.make_async_copy(fp_hbm, fpt, p_sem.at[1])
    vp_load.start()
    load(0).start()
    fp_load.start()
    for s in range(1, row_chunks):
        load(s).start()

    def vox_peer(d):
        return (mv // side + d // side) % (nv // side) * side + (mv + d) % side

    def frm_peer(d):
        return (mf // cores + d // cores) % (nf // cores) * cores + (mf + d) % cores

    vox_order, frm_order = far_first(nv, side), far_first(nf, cores)
    barrier = pltpu.get_barrier_semaphore()
    for d in vox_order:
        pl.semaphore_signal(barrier, inc=1, device_id={"vox": vox_peer(d)}, device_id_type=MESH)
    for d in frm_order:
        pl.semaphore_signal(barrier, inc=1, device_id={"frm": frm_peer(d)}, device_id_type=MESH)

    def to(axis, src, dst, sems, it, target):
        return pltpu.make_async_remote_copy(
            src_ref=src, dst_ref=dst, send_sem=sems.at[it, 0], recv_sem=sems.at[it, 1],
            device_id={axis: target}, device_id_type=MESH,
        )

    def f_to(it, owner):
        slot = (owner // side - mv // side + nv // side) % (nv // side) * side + (owner - mv + nv) % side - 1
        return to("vox", f_send.at[it, owner], f_recv.at[it, slot], f_sem, it, owner)

    def v_to(it, owner):
        slot = (owner // cores - mf // cores + nf // cores) % (nf // cores) * cores + (owner - mf + nf) % cores - 1
        return to("frm", v_send.at[it, owner], v_recv.at[it, slot], v_sem, it, owner)

    def whole(kind, it):
        if kind == "f":
            return to("vox", f_recv.at[it], f_recv.at[it], f_sem, it, vox_peer(1))
        if kind == "fg":
            part = ft_full.at[it, pl.ds(0, nv - 1)]
            return to("vox", part, part, fg_sem, it, vox_peer(1))
        if kind == "v":
            return to("frm", v_recv.at[it], v_recv.at[it], v_sem, it, frm_peer(1))
        if kind == "vg":
            part = vt_full.at[it, pl.ds(0, nf - 1)]
            return to("frm", part, part, vg_sem, it, frm_peer(1))
        if kind == "ta":
            return to("frm", t_recv.at[it], t_recv.at[it], ta_sem, it, frm_peer(1))
        return to("vox", t_wide.at[it], t_wide.at[it], tb_sem, it, vox_peer(1))

    for it in range(ITERS):
        fc = nv if it else fc_first
        rows, row_chunks = fb * fc, nv // fc
        src = m_buf if it == 0 else c_buf

        def frame_step(s, carry):
            c = row_chunk(s, fc)
            if it == 0:
                load(s).wait()
            else:
                left = jnp.concatenate([ft_full[it - 1, fc * c + i] for i in range(fc)], axis=1).T
                for j in range(voxels // WIDE):
                    at = (rows_of(c, rows), pl.ds(j * WIDE, WIDE))
                    low = mm(left, w_buf[:, at[1]], NN)
                    floor, roof = (low - cutoff).astype(BF16), (low + cutoff).astype(BF16)
                    c_buf[at] = jnp.minimum(jnp.maximum(m_buf[at], floor), roof)
            ft = mm(vpt[...], src[rows_of(c, rows), :], NT)
            high, low_part = split(ft)
            for i in range(fc):
                f_send[it, fc * c + i] = high[:, i * fb : (i + 1) * fb]
            probe = fpt[:, rows_of(c, rows)]
            t_acc[...] += mm(high, probe, NT) + mm(low_part, probe, NT)
            if it > 0:
                for i in range(fc):
                    owner = fc * c + i

                    @pl.when(owner != mv)
                    def _():
                        f_to(it, owner).start()

            return carry

        t_acc[...] = jnp.zeros_like(t_acc)
        if it == 0:
            vp_load.wait()
            fp_load.wait()
        lax.fori_loop(0, row_chunks, frame_step, 0)

        t_mine[it] = jnp.concatenate([t_acc[:HALF, :], t_acc[HALF:, :]], axis=1)
        if it == 0:
            pl.semaphore_wait(barrier, nv + nf - 2)
        for d in frm_order:
            to("frm", t_mine.at[it], t_recv.at[it, d - 1], ta_sem, it, frm_peer(d)).start()
        if it == 0:
            for d in vox_order:
                f_to(it, vox_peer(d)).start()

        def voxel_step(s, carry):
            c = lax.rem(mf // vc + 1 + s, column_chunks)
            at = pl.ds(pl.multiple_of(c * columns, columns), columns)
            vt = mm(fpt[...], src[:, at], NN).astype(BF16)
            for i in range(vc):
                owner = vc * c + i
                v_send[it, owner] = vt[:, i * vb : (i + 1) * vb]

                @pl.when(owner != mf)
                def _():
                    v_to(it, owner).start()

            return carry

        lax.fori_loop(0, column_chunks, voxel_step, 0)

        whole("ta", it).wait_recv()
        part = t_mine[it]
        for d in range(nf - 1):
            part = part + t_recv[it, d]
        t_sum[it] = part
        for d in vox_order:
            to("vox", t_sum.at[it], t_wide.at[it, d - 1], tb_sem, it, vox_peer(d)).start()

        whole("f", it).wait_recv()
        share = f_send[it, mv].astype(F32)
        for d in range(nv - 1):
            share = share + f_recv[it, d].astype(F32)
        ft_full[it, mv] = share.astype(BF16)
        for d in vox_order:
            to("vox", ft_full.at[it, mv], ft_full.at[it, mv], fg_sem, it, vox_peer(d)).start()

        whole("v", it).wait_recv()
        share = v_send[it, mf].astype(F32)
        for d in range(nf - 1):
            share = share + v_recv[it, d].astype(F32)
        vt_full[it, mf] = share.astype(BF16)
        for d in frm_order:
            to("frm", vt_full.at[it, mf], vt_full.at[it, mf], vg_sem, it, frm_peer(d)).start()

        whole("tb", it).wait_recv()
        part = t_sum[it]
        for d in range(nv - 1):
            part = part + t_wide[it, d]
        lanes = lax.broadcasted_iota(jnp.int32, part.shape, 1)
        left_half = jnp.where(lanes < RANK, part, 0.0)
        right_half = pltpu.roll(jnp.where(lanes < RANK, 0.0, part), RANK, 1)
        mixer = mixer_of(jnp.concatenate([left_half, right_half], axis=0), keep)
        high, low_part = split(mixer)
        both = jnp.where(lax.broadcasted_iota(jnp.int32, mixer.shape, 1) < RANK, high.astype(F32), pltpu.roll(low_part.astype(F32), RANK, 1))
        mix[...] = both.astype(BF16)

        whole("vg", it).wait_recv()
        for b in range(nf):
            right = vt_full[it, b]
            w = mm(mix[...], jnp.concatenate([right, right], axis=0), NN)
            w_buf[:, b * vb : (b + 1) * vb] = w.astype(BF16)
        whole("fg", it).wait_recv()

    ft_out[...] = ft_full[ITERS - 1]
    for it in range(ITERS):
        for kind in ("f", "fg", "v", "vg", "ta", "tb"):
            whole(kind, it).wait_send()


def output_kernel(per, m_ref, ft_ref, w_ref, low_hbm, sparse_hbm, low_buf, sparse_buf, sems):
    slots, rows, voxels = low_buf.shape
    steps = ft_ref.shape[0] // per

    def copies(i):
        at, k = pl.ds(i * rows, rows), i % slots
        return (
            pltpu.make_async_copy(low_buf.at[k], low_hbm.at[at], sems.at[0, k]),
            pltpu.make_async_copy(sparse_buf.at[k], sparse_hbm.at[at], sems.at[1, k]),
        )

    for i in range(steps):
        k = i % slots
        if i >= slots:
            for copy in copies(i - slots):
                copy.wait()
        left = jnp.concatenate([ft_ref[per * i + q] for q in range(per)], axis=1).T
        for j in range(voxels // WIDE):
            cols = pl.ds(j * WIDE, WIDE)
            low = mm(left, w_ref[:, cols], NN)
            rest = m_ref[pl.ds(i * rows, rows), cols].astype(F32) - low
            low_buf[k, :, cols] = low.astype(BF16)
            sparse_buf[k, :, cols] = (rest - jnp.clip(rest, -cutoff, cutoff)).astype(BF16)
        for copy in copies(i):
            copy.start()
    for i in range(steps - slots, steps):
        for copy in copies(i):
            copy.wait()


def solution(mesh):
    nv, nf = mesh.shape["vox"], mesh.shape["frm"]

    def on_device(movie_matrix, voxel_probe, frame_probe):
        frames, voxels = movie_matrix.shape
        fb, vb = frames // nv, voxels // nf
        vmem = pl.BlockSpec(memory_space=pltpu.VMEM)
        hbm = pl.BlockSpec(memory_space=pltpu.HBM)
        dma = pltpu.SemaphoreType.DMA
        fc, vc = nv // 2, nf // 2
        movie, ft, w = pl.pallas_call(
            functools.partial(sketch_kernel, nv, nf, 4, 2, fc, vc),
            out_shape=(
                jax.ShapeDtypeStruct((frames, voxels), BF16),
                jax.ShapeDtypeStruct((nv, RANK, fb), BF16),
                jax.ShapeDtypeStruct((RANK, voxels), BF16),
            ),
            in_specs=[hbm, hbm, hbm],
            out_specs=(vmem, vmem, vmem),
            scratch_shapes=[
                pltpu.VMEM((frames, voxels), BF16),
                pltpu.VMEM((RANK, voxels), BF16),
                pltpu.VMEM((RANK, frames), BF16),
                pltpu.VMEM((ITERS, nv, RANK, fb), BF16),
                pltpu.VMEM((ITERS, nv - 1, RANK, fb), BF16),
                pltpu.VMEM((ITERS, nv, RANK, fb), BF16),
                pltpu.VMEM((ITERS, nf, RANK, vb), BF16),
                pltpu.VMEM((ITERS, nf - 1, RANK, vb), BF16),
                pltpu.VMEM((ITERS, nf, RANK, vb), BF16),
                pltpu.VMEM((RANK, RANK), F32),
                pltpu.VMEM((ITERS, HALF, LANES), F32),
                pltpu.VMEM((ITERS, nf - 1, HALF, LANES), F32),
                pltpu.VMEM((ITERS, HALF, LANES), F32),
                pltpu.VMEM((ITERS, nv - 1, HALF, LANES), F32),
                pltpu.VMEM((RANK, LANES), BF16),
                pltpu.VMEM((RANK // SUB, SUB, SUB, LANES), F32),
                dma((nv // fc,)),
                dma((2,)),
            ]
            + [dma((ITERS, 2))] * 6,
            compiler_params=pltpu.CompilerParams(
                collective_id=0, has_side_effects=True, vmem_limit_bytes=40 * 1024 * 1024
            ),
            name="sketches",
        )(
            movie_matrix,
            pltpu.with_memory_space_constraint(voxel_probe.T, pltpu.HBM),
            pltpu.with_memory_space_constraint(frame_probe.T, pltpu.HBM),
        )
        per, slots = 2, 4
        return pl.pallas_call(
            functools.partial(output_kernel, per),
            out_shape=(
                jax.ShapeDtypeStruct((frames, voxels), BF16),
                jax.ShapeDtypeStruct((frames, voxels), BF16),
            ),
            in_specs=[vmem, vmem, vmem],
            out_specs=(hbm, hbm),
            scratch_shapes=[pltpu.VMEM((slots, per * fb, voxels), BF16)] * 2 + [dma((2, slots))],
            compiler_params=pltpu.CompilerParams(vmem_limit_bytes=24 * 1024 * 1024),
            name="outputs",
        )(movie, ft, w)

    return jax.shard_map(
        on_device,
        mesh=mesh,
        in_specs=(P("frm", "vox"), P("vox", None), P("frm", None)),
        out_specs=(P("frm", "vox"), P("frm", "vox")),
        check_vma=False,
    )
```
